32 devices in a mesh: space: 4 (over y, x), mode: 8 (over z, core).
Axes of the slice: x: 2, y: 2, z: 4, core: 2. Of those that a mesh axis runs over, the one named last changes fastest.
Arguments:
- source_field: float32 [8, 4, 128, 2048], P('space', None, None, 'mode'), may hold values from -6 to 6
- mean_operator: float32 [8, 4, 128, 896], P('space'), may hold values from -0.109375 to 0.109375
- field_operators: float32 [4, 8, 4, 128, 896], P(None, 'space'), may hold values from -0.078125 to 0.078125
- adjacency: int32 [8, 4, 4], P('space'), may hold values from 0 to 3
- mode_masks: int32 [4], replicated, may hold values from 256 to 1024, as said below
Outputs:
- solution_field: float32 [8, 4, 128, 2048], P('space', None, None, 'mode')
- residual: float32 [8, 4, 128, 2048], P('space', None, None, 'mode')
The draws below stay inside these ranges and needn't reach their ends.
Inputs may be any that keep to these rules, and one draw needn't show every extreme that they name: `mode_masks`: each value is 256 times a power of two, at most 1024, and every such value belongs to at least one field.
All inputs are finite; a program needn't handle non-finite values.
Results may differ from the reference program's by a relative error of at most 0.0001.
Values sent between devices are 32-bit elements; how exact they have to be, the bound alone decides.
A program may use at most 128 MiB of HBM per device.

```python
import jax
import jax.numpy as jnp
from jax import lax

BLK = 128
MODE_DEV = 256
MODES = 2048
NF = 4
FACE = 4
LAYERS = 8
DEGREE = 4


def draw_mode_masks(key, part):
    bit_count = (MODES // MODE_DEV).bit_length() - 1
    order = jax.random.permutation(jax.random.fold_in(key, 11), NF)
    extra = jax.random.randint(jax.random.fold_in(key, 12), (NF,), 0, bit_count)
    slots = jnp.arange(NF, dtype=jnp.int32)
    slot_bits = jnp.where(slots < bit_count, slots, extra)
    field_bits = slot_bits[order]
    return (MODE_DEV * jnp.left_shift(jnp.ones((NF,), jnp.int32), field_bits)).astype(jnp.int32)


def with_ends(values, rng, low, largest):
    shape = values.shape
    index_at = [jax.random.randint(jax.random.fold_in(rng, axis), (), 0, shape[axis]) for axis in range(len(shape))]
    values = values.at[tuple(index_at)].set(low)
    longest = shape.index(max(shape))
    index_at[longest] = (index_at[longest] + 1) % shape[longest]
    return values.at[tuple(index_at)].set(largest)


def level_of(key, shape, pieces, low, top_value):
    loudness, own = 1.0, jax.random.fold_in(key, 6)
    for axis_at, shards_of in pieces:
        draws = jnp.exp(jax.random.uniform(jax.random.fold_in(own, axis_at), (shards_of,), jnp.float32, low / len(pieces), top_value / len(pieces)))
        loudness = loudness * jnp.repeat(draws, shape[axis_at] // shards_of).reshape([-1 if axis == axis_at else 1 for axis in range(len(shape))])
    return loudness


def gaussian(own_key, shape, deviation, limit, split=(), kind=jnp.bfloat16):
    factor_of = level_of(own_key, shape, split, -0.22, 0.18) if split else 1.0
    array = jax.random.normal(own_key, shape, jnp.float32) * deviation * factor_of
    return jnp.minimum(jnp.maximum(array, -limit), limit).astype(kind)


def setup_inputs(seed: int = 0) -> dict:
    streams_of = jax.random.split(jax.random.key(seed), 6)
    return {
        "source_field": gaussian(streams_of[0], (LAYERS, FACE, BLK, MODES), 1.0, 6.0, ((0, 4), (3, 8)), jnp.float32),
        "mean_operator": gaussian(streams_of[1], (LAYERS, FACE, BLK, 7 * BLK), 0.007, 0.109375, ((0, 4),), jnp.float32),
        "field_operators": gaussian(streams_of[2], (NF, LAYERS, FACE, BLK, 7 * BLK), 0.005, 0.078125, ((1, 4),), jnp.float32),
        "adjacency": with_ends(jax.random.randint(streams_of[3], (LAYERS, FACE, 4), 0, FACE), jax.random.fold_in(streams_of[3], 1), 0, FACE - 1).astype(jnp.int32),
        "mode_masks": draw_mode_masks(jax.random.fold_in(streams_of[5], 71), 0),
    }


coupling_coef = 0.5773502691896258
theta_value = 1.0
delta_value = 0.7


def operate_on(field, mean_operator, field_operators, adjacency, mode_masks):
    padded = jnp.pad(field, ((1, 1), (0, 0), (0, 0), (0, 0)))
    mode_index = jnp.arange(field.shape[3], dtype=jnp.int32)

    def one_layer(layer_index):
        window = lax.dynamic_slice_in_dim(padded, layer_index, 3, 0)
        centre = window[1]
        neighbours = adjacency[layer_index]
        in_layer = centre[neighbours]
        stacked = jnp.concatenate([centre[:, None], window[0][:, None], window[2][:, None], in_layer], axis=1)
        columns = stacked.reshape(FACE, 7 * BLK, field.shape[3])
        result = centre + jnp.einsum("fij,fjm->fim", mean_operator[layer_index], columns, precision=lax.Precision.HIGHEST)
        for field_number in range(NF):
            term = jnp.einsum("fij,fjm->fim", field_operators[field_number, layer_index], columns, precision=lax.Precision.HIGHEST)
            partner = jnp.bitwise_xor(mode_index, mode_masks[field_number])
            result = result + coupling_coef * jnp.take(term, partner, axis=2)
        return result

    return lax.map(one_layer, jnp.arange(LAYERS, dtype=jnp.int32))


def reference(source_field, mean_operator, field_operators, adjacency, mode_masks):
    sigma_value = theta_value / delta_value
    solution_field = jnp.zeros_like(source_field)
    residual = source_field
    direction = source_field / theta_value
    ratio_now = jnp.asarray(1.0 / sigma_value, dtype=jnp.float32)

    def iterate_once(count, carry):
        solution_field, residual, direction, ratio_now = carry
        solution_field = solution_field + direction
        residual = residual - operate_on(direction, mean_operator, field_operators, adjacency, mode_masks)
        ratio_new = 1.0 / (2.0 * sigma_value - ratio_now)
        direction = ratio_new * ratio_now * direction + (2.0 * ratio_new / delta_value) * residual
        return solution_field, residual, direction, ratio_new

    solution_field, residual, direction, ratio_now = lax.fori_loop(0, DEGREE, iterate_once, (solution_field, residual, direction, ratio_now))
    return solution_field, residual
```

```python
import functools

import jax
import jax.numpy as jnp
from jax import lax
from jax.experimental import pallas as pl
from jax.experimental.pallas import tpu as pltpu
from jax.sharding import PartitionSpec as P

DEGREE = 4
COUPLING = 0.5773502691896258
THETA = 1.0
DELTA = 0.7
CHUNKS = 4
GROUP = 2
LAG = 4
LEAD = 3
SLOTS = 4
RELAYED_GROUP = 1
VMEM_LIMIT = 56_000_000
MESH = pl.DeviceIdType.MESH


def prepare(raw, e, slot, modes_dev, adj_ref, mask_ref, w_hi, w_lo):
    face, blk = w_hi.shape[1], raw.shape[2]
    layer, f = e // face, lax.rem(e, face)
    for op in range(w_hi.shape[3] // blk):
        if op == 0:
            weights = [None]
        else:
            weights = [
                jnp.where(mask_ref[j] == modes_dev * (1 << (op - 1)), COUPLING, 0.0).astype(jnp.float32)
                for j in range(raw.shape[1] - 1)
            ]

        def block(s):
            lanes = slice(s * blk, (s + 1) * blk)
            if op == 0:
                return raw[slot, 0, :, lanes]
            total = weights[0] * raw[slot, 1, :, lanes]
            for j in range(1, len(weights)):
                total = total + weights[j] * raw[slot, 1 + j, :, lanes]
            return total

        own = block(0)
        sides = [block(3 + s) for s in range(adj_ref.shape[2])]
        parts = []
        for g in range(face):
            total = jnp.where(f == g, 1.0, 0.0).astype(jnp.float32) * own
            for s, side in enumerate(sides):
                total = total + jnp.where(adj_ref[layer, f, s] == g, 1.0, 0.0).astype(jnp.float32) * side
            parts.append(total)
        parts += [block(1), block(2)]
        for at, part in enumerate(parts):
            part = part.T
            high = part.astype(jnp.bfloat16)
            low = (part - high.astype(jnp.float32)).astype(jnp.bfloat16)
            w_hi[layer, f, at * blk : (at + 1) * blk, op * blk : (op + 1) * blk] = high
            w_lo[layer, f, at * blk : (at + 1) * blk, op * blk : (op + 1) * blk] = low


def schedule(chunks):
    steps = []
    group = min(GROUP, chunks)
    for turn in range(DEGREE + LAG * (chunks // group - 1)):
        for place in range(group):
            for c in range(place, chunks, group):
                t = turn - LAG * (c // group)
                if 0 <= t < DEGREE:
                    steps.append((t, c))
    items = []
    for at, step in enumerate(steps):
        for c in range(chunks):
            if max(steps.index((0, c)) - (LEAD if c >= group else 0), 0) == at:
                items.append((-1, c))
        items.append(step)
    plan = []
    for at, item in enumerate(items):
        ahead = items[at + 1] if at + 1 < len(items) else (-1, 0)
        if ahead[0] < 0 and at + 2 < len(items) and item[0] < 0:
            ahead = items[at + 2]
        if any(ahead == done[2:] for done in plan) or ahead[0] < 0:
            ahead = (-1, 0)
        plan.append(item + ahead)
    missing = [item for item in items if item[0] >= 0 and item not in [done[2:] for done in plan]]
    assert not missing, missing
    return plan


def solve_kernel(
    peers, spaces, chunks, modes_dev, source, mean, fields, adj, masks, x_out, r_out,
    raw, w_hi, w_lo, direction, res, x, split, acc, halo_low, halo_up, relay, stage, src, x_land, r_land,
    w_sem, stage_sem, own_sem, in_send, in_recv, low_send, low_recv, up_send, up_recv,
    relay_send, relay_recv, forward_send, forward_recv, out_send, out_recv, own_out,
):
    layers, face, inner, width = w_hi.shape
    blk = inner // (face + 2)
    bits = peers.bit_length() - 1
    rows = direction.shape[4]
    lc = rows // peers
    me = lax.axis_index("mode")
    s = lax.axis_index("space")
    has_low = s > 0
    has_up = s < spaces - 1
    relayed = spaces >= 4 and spaces % 2 == 0 and face % 2 == 0
    groups = 2 if face % 2 == 0 else 1
    per = face // groups
    odd = lax.rem(s, 2) == 1
    even = jnp.logical_not(odd)
    both = jnp.logical_and
    elements = layers * face

    def loads(e):
        slot = lax.rem(e, SLOTS)
        l, f = e // face, lax.rem(e, face)
        return (
            pltpu.make_async_copy(mean.at[l, f], raw.at[slot, 0], w_sem.at[slot, 0]),
            pltpu.make_async_copy(fields.at[:, l, f], raw.at[slot, pl.ds(1, fields.shape[0])], w_sem.at[slot, 1]),
        )

    fetch = pltpu.make_async_copy(source, stage, stage_sem.at[0])
    fetch.start()
    for e in range(min(SLOTS, elements)):
        for load in loads(e):
            load.start()

    barrier = pltpu.get_barrier_semaphore()
    for k in range(1, peers):
        pl.semaphore_signal(barrier, inc=1, device_id={"mode": lax.rem(me + k, peers)}, device_id_type=MESH)

    @pl.when(has_low)
    def _():
        pl.semaphore_signal(barrier, inc=1, device_id={"space": s - 1}, device_id_type=MESH)

    @pl.when(has_up)
    def _():
        pl.semaphore_signal(barrier, inc=1, device_id={"space": s + 1}, device_id_type=MESH)

    expected = peers - 1 + has_low.astype(jnp.int32) + has_up.astype(jnp.int32)
    if relayed:
        far_low, far_up = s >= 2, s < spaces - 2
        expected = expected + far_low.astype(jnp.int32) + far_up.astype(jnp.int32)

        @pl.when(far_low)
        def _():
            pl.semaphore_signal(barrier, inc=1, device_id={"space": s - 2}, device_id_type=MESH)

        @pl.when(far_up)
        def _():
            pl.semaphore_signal(barrier, inc=1, device_id={"space": s + 2}, device_id_type=MESH)

    bands = min(chunks, max(modes_dev // 128, 1))
    band = modes_dev // bands
    in_band = chunks // bands
    fetch.wait()
    for n in range(bands):
        modes = slice(n * band, (n + 1) * band)
        for l in range(layers):
            for f in range(face):
                src[l, f, modes] = stage[l, f, :, modes].T * (1.0 / THETA)

    with jax.named_scope('barrier'):
        pl.semaphore_wait(barrier, expected)

    def slab(ref, c, h):
        return ref.at[c, :, :, pl.ds(pl.multiple_of(h * lc, lc), lc), :]

    def piece(ref, c, h):
        return ref.at[:, :, pl.ds(pl.multiple_of((c * peers + h) * lc, lc), lc), :]

    def in_copy(c, k):
        to = lax.rem(me + k, peers)
        return pltpu.make_async_remote_copy(
            src_ref=piece(src, c, to), dst_ref=slab(direction.at[0], c, me),
            send_sem=in_send.at[0], recv_sem=in_recv.at[c],
            device_id={"mode": to}, device_id_type=MESH,
        )

    def whole(ref, count, send_sem, recv_sem):
        part = ref.at[:, :, pl.ds(0, count), :]
        return pltpu.make_async_remote_copy(
            src_ref=part, dst_ref=part, send_sem=send_sem, recv_sem=recv_sem,
            device_id={"mode": lax.rem(me + 1, peers)}, device_id_type=MESH,
        )

    def own_copy(c):
        return pltpu.make_async_copy(piece(src, c, me), slab(direction.at[0], c, me), own_sem.at[c])

    def to_low(t, c, g):
        part = pl.ds(g * per, per)
        return pltpu.make_async_remote_copy(
            src_ref=direction.at[lax.rem(t, 2), c, 0, part], dst_ref=halo_up.at[t, c, part],
            send_sem=low_send.at[lax.rem(t, 2), c, g], recv_sem=up_recv.at[lax.rem(t, 2), c, g],
            device_id={"space": s - 1}, device_id_type=MESH,
        )

    def to_up(t, c, g):
        part = pl.ds(g * per, per)
        return pltpu.make_async_remote_copy(
            src_ref=direction.at[lax.rem(t, 2), c, layers - 1, part], dst_ref=halo_low.at[t, c, part],
            send_sem=up_send.at[lax.rem(t, 2), c, g], recv_sem=low_recv.at[lax.rem(t, 2), c, g],
            device_id={"space": s + 1}, device_id_type=MESH,
        )

    def to_relay(t, c, layer, offset):
        return pltpu.make_async_remote_copy(
            src_ref=direction.at[lax.rem(t, 2), c, layer, pl.ds(RELAYED_GROUP * per, per)], dst_ref=relay.at[t, c],
            send_sem=relay_send.at[lax.rem(t, 2), c], recv_sem=relay_recv.at[lax.rem(t, 2), c],
            device_id={"space": s + offset}, device_id_type=MESH,
        )

    def forward(t, c, halo, offset):
        return pltpu.make_async_remote_copy(
            src_ref=relay.at[t, c], dst_ref=halo.at[t, c, pl.ds(RELAYED_GROUP * per, per)],
            send_sem=forward_send.at[0], recv_sem=forward_recv.at[lax.rem(t, 2), c],
            device_id={"space": s + offset}, device_id_type=MESH,
        )

    def halo_each(t, c, g, act):
        hop = relayed and g == RELAYED_GROUP

        @pl.when(both(even, has_low))
        def _():
            act(to_relay(t, c, 0, -2) if hop else to_low(t, c, g))

        @pl.when(both(odd, has_up))
        def _():
            act(to_relay(t, c, layers - 1, 2) if hop else to_up(t, c, g))

        @pl.when(both(odd, has_low))
        def _():
            act(to_low(t, c, g))

        @pl.when(both(even, has_up))
        def _():
            act(to_up(t, c, g))

    def halo_start(t, c, g):
        halo_each(t, c, g, lambda copy: copy.start())

    def halo_sent(t, c):
        for g in range(groups):
            halo_each(t, c, g, lambda copy: copy.wait_send())

    def forward_each(t, c, act):
        if relayed:

            @pl.when(both(odd, s >= 3))
            def _():
                act(forward(t, c, halo_low, -1))

            @pl.when(both(even, s < spaces - 3))
            def _():
                act(forward(t, c, halo_up, 1))

    def halo_forward(t, c):
        if relayed:

            @pl.when(jnp.logical_or(both(odd, s >= 3), both(even, s < spaces - 3)))
            def _():
                to_relay(t, c, 0, jnp.where(odd, -1, 1)).wait_recv()

            forward_each(t, c, lambda copy: copy.start())

    def halo_arrived(t, c, g):
        hop = relayed and g == RELAYED_GROUP

        @pl.when(both(odd, has_low))
        def _():
            to_up(t, c, g).wait_recv()

        @pl.when(both(even, has_up))
        def _():
            to_low(t, c, g).wait_recv()

        @pl.when(both(even, has_low))
        def _():
            (forward(t, c, halo_low, -1) if hop else to_up(t, c, g)).wait_recv()

        @pl.when(both(odd, has_up))
        def _():
            (forward(t, c, halo_up, 1) if hop else to_low(t, c, g)).wait_recv()

    def out_start(which, ref, land, c):
        for k in range(1, peers):
            to = lax.rem(me + k, peers)
            pltpu.make_async_remote_copy(
                src_ref=slab(ref, c, to), dst_ref=piece(land, c, me),
                send_sem=out_send.at[which], recv_sem=out_recv.at[which, c // in_band],
                device_id={"mode": to}, device_id_type=MESH,
            ).start()
        pltpu.make_async_copy(slab(ref, c, me), piece(land, c, me), own_out.at[which, c // in_band]).start()

    def out_finish(which, land, out, n):
        count = in_band * (peers - 1) * lc
        whole(land, count, out_send.at[which], out_recv.at[which, n]).wait_recv()
        own = land.at[:, :, pl.ds(0, in_band * lc), :]
        pltpu.make_async_copy(own, own, own_out.at[which, n]).wait()
        modes = slice(n * band, (n + 1) * band)
        for l in range(layers):
            for f in range(face):
                out[l, f, :, modes] = land[l, f, modes].T

    for c in range(chunks):
        for k in range(1, peers):
            in_copy(c, k).start()
        own_copy(c).start()

    @pl.when(jnp.logical_not(has_low))
    def _():
        halo_low[...] = jnp.zeros_like(halo_low)

    @pl.when(jnp.logical_not(has_up))
    def _():
        halo_up[...] = jnp.zeros_like(halo_up)

    def land(c):
        own_copy(c).wait()
        whole(src, (peers - 1) * lc, in_send.at[0], in_recv.at[c]).wait_recv()
        for g in range(groups):
            halo_start(0, c, g)

    items = schedule(chunks)

    def build(e, carry):
        for load in loads(e):
            load.wait()
        prepare(raw, e, lax.rem(e, SLOTS), modes_dev, adj, masks, w_hi, w_lo)

        @pl.when(e + SLOTS < elements)
        def _():
            for load in loads(e + SLOTS):
                load.start()

        return carry

    with jax.named_scope('build'):
        lax.fori_loop(0, elements, build, 0)

    def halves(value):
        high = value.astype(jnp.bfloat16)
        return high, (value - high.astype(jnp.float32)).astype(jnp.bfloat16)

    def product(a, l, f, lo, hi):
        def dot(left, right):
            return lax.dot_general(left, right, (((1,), (0,)), ((), ())), preferred_element_type=jnp.float32)

        y = dot(a, w_hi[l, f, lo:hi])
        return y[:rows] + y[rows:] + dot(a[:rows], w_lo[l, f, lo:hi])

    def keep_split(c, l, f, value):
        high, low = halves(value)
        split[c, l, :rows, f * blk : (f + 1) * blk] = high
        split[c, l, rows:, f * blk : (f + 1) * blk] = low

    sigma = THETA / DELTA
    last = (DEGREE - 1) % 2
    ratios = [1.0 / sigma]
    for _ in range(DEGREE):
        ratios.append(1.0 / (2.0 * sigma - ratios[-1]))

    def item(i):
        found = [jnp.int32(-1)] * 4
        for at, entry in enumerate(items):
            found = [jnp.where(i == at, value, old) for value, old in zip(entry, found)]
        return found

    def side(c, l, f, halo, t):
        if 0 <= l < layers:
            return split[c, l, :, f * blk : (f + 1) * blk]
        return jnp.concatenate(halves(halo[t, c, f]), axis=0)

    def advance(i, carry):
        t, c, t_next, c_next = item(i)

        @pl.when(t < 0)
        def _():
            with jax.named_scope('land'):
                land(c)

            for l in range(layers):
                for f in range(face):
                    d = direction[0, c, l, f]
                    res[c, l, f] = d
                    x[0, c, l, f] = d
                    keep_split(c, l, f, d)

        now = lax.rem(t + 2, 2)
        keep, add = jnp.float32(0.0), jnp.float32(0.0)
        for at in range(DEGREE - 1):
            keep = jnp.where(t == at, jnp.float32(ratios[at + 1] * ratios[at]), keep)
            add = jnp.where(t == at, jnp.float32(2.0 * ratios[at + 1] / DELTA), add)

        for g in range(groups):

            @pl.when(t >= 0)
            def _():
                with jax.named_scope(f'wait{g}'):
                    halo_arrived(t, c, g)

                if g == 0:

                    @pl.when(t > 0)
                    def _():
                        halo_sent(t - 1, c)

                for f in range(g * per, (g + 1) * per):
                    ys = []
                    for l in range(layers):
                        a = jnp.concatenate([side(c, l - 1, f, halo_low, t), side(c, l + 1, f, halo_up, t)], axis=1)
                        ys.append(acc[c, l, f] + product(a, l, f, face * blk, inner))
                    for l, y in enumerate(ys):
                        d = direction[now, c, l, f]
                        total = d + y[:, :blk]
                        for b in range(bits):
                            term = y[:, (b + 1) * blk : (b + 2) * blk]
                            total = total + jnp.concatenate(
                                [term[(h ^ (1 << b)) * lc : ((h ^ (1 << b)) + 1) * lc] for h in range(peers)], axis=0
                            )
                        r = res[c, l, f] - total
                        res[c, l, f] = r
                        d_new = keep * d + add * r
                        direction[1 - now, c, l, f] = d_new
                        x[1 - now, c, l, f] = x[now, c, l, f] + d_new
                        keep_split(c, l, f, d_new)

                @pl.when(t < DEGREE - 1)
                def _():
                    halo_start(t + 1, c, g)

        @pl.when(t == DEGREE - 2)
        def _():
            out_start(0, x.at[last], x_land, c)

        @pl.when(t == DEGREE - 1)
        def _():
            out_start(1, res, r_land, c)

        @pl.when(t < DEGREE - 1)
        def _():
            for l in range(layers):
                a = split[c, l]
                for f in range(face):
                    acc[c, l, f] = product(a, l, f, 0, face * blk)

        @pl.when(t_next >= 0)
        def _():
            with jax.named_scope('fwd'):
                halo_forward(t_next, c_next)

        return carry

    lax.fori_loop(0, len(items), advance, 0)

    with jax.named_scope('sent'):
        for c in range(chunks):
            halo_sent(DEGREE - 1, c)
        everything = (peers - 1) * chunks * lc
        whole(src, everything, in_send.at[0], in_recv.at[0]).wait_send()
        if relayed:

            @pl.when(jnp.logical_or(both(odd, s >= 3), both(even, s < spaces - 3)))
            def _():
                pltpu.make_async_remote_copy(
                    src_ref=relay, dst_ref=relay, send_sem=forward_send.at[0], recv_sem=forward_recv.at[0, 0],
                    device_id={"space": s + jnp.where(odd, -1, 1)}, device_id_type=MESH,
                ).wait_send()

    for n in range(bands):
        with jax.named_scope(f'finx{n}'):
            out_finish(0, x_land, x_out, n)
        with jax.named_scope(f'finr{n}'):
            out_finish(1, r_land, r_out, n)
    with jax.named_scope('end'):
        for which, land, out in ((0, x_land, x_out), (1, r_land, r_out)):
            whole(land, everything, out_send.at[which], out_recv.at[which, 0]).wait_send()


def deliver(x, r, x_out, r_out, sem):
    copies = [pltpu.make_async_copy(x, x_out, sem.at[0]), pltpu.make_async_copy(r, r_out, sem.at[1])]
    for copy in copies:
        copy.start()
    for copy in copies:
        copy.wait()


def per_device(peers, spaces, source_field, mean_operator, field_operators, adjacency, mode_masks):
    layers, face, blk, modes_dev = source_field.shape
    bits = peers.bit_length() - 1
    chunks = CHUNKS
    while modes_dev % (peers * chunks * 8):
        chunks //= 2
    rows = modes_dev // chunks
    groups = 2 if face % 2 == 0 else 1
    weights = pltpu.VMEM((layers, face, (face + 2) * blk, (bits + 1) * blk), jnp.bfloat16)
    out = pltpu.VMEM(source_field.shape, jnp.float32)
    landing = pltpu.VMEM((layers, face, modes_dev, blk), jnp.float32)
    bands = min(chunks, max(modes_dev // 128, 1))
    field = (chunks, layers, face, rows, blk)
    halo = pltpu.VMEM((DEGREE, chunks, face, rows, blk), jnp.float32)
    dma = pltpu.SemaphoreType.DMA
    x, r = pl.pallas_call(
        functools.partial(solve_kernel, peers, spaces, chunks, modes_dev),
        in_specs=[
            pl.BlockSpec(memory_space=pl.ANY),
            pl.BlockSpec(memory_space=pl.ANY),
            pl.BlockSpec(memory_space=pl.ANY),
            pl.BlockSpec(memory_space=pltpu.SMEM),
            pl.BlockSpec(memory_space=pltpu.SMEM),
        ],
        out_specs=(pl.BlockSpec(memory_space=pltpu.VMEM), pl.BlockSpec(memory_space=pltpu.VMEM)),
        out_shape=(out, out),
        scratch_shapes=[
            pltpu.VMEM((SLOTS, 1 + field_operators.shape[0]) + mean_operator.shape[2:], jnp.float32),
            weights,
            weights,
            pltpu.VMEM((2,) + field, jnp.float32),
            pltpu.VMEM(field, jnp.float32),
            pltpu.VMEM((2,) + field, jnp.float32),
            pltpu.VMEM((chunks, layers, 2 * rows, face * blk), jnp.bfloat16),
            pltpu.VMEM((chunks, layers, face, rows, (bits + 1) * blk), jnp.float32),
            halo,
            halo,
            pltpu.VMEM((DEGREE, chunks, face // groups, rows, blk), jnp.float32),
            pltpu.VMEM(source_field.shape, jnp.float32),
            landing,
            landing,
            landing,
            dma((SLOTS, 2)),
            dma((1,)),
            dma((chunks,)),
            dma((1,)),
            dma((chunks,)),
            dma((2, chunks, groups)),
            dma((2, chunks, groups)),
            dma((2, chunks, groups)),
            dma((2, chunks, groups)),
            dma((2, chunks)),
            dma((2, chunks)),
            dma((1,)),
            dma((2, chunks)),
            dma((2,)),
            dma((2, bands)),
            dma((2, bands)),
        ],
        compiler_params=pltpu.CompilerParams(
            collective_id=0, has_side_effects=True, vmem_limit_bytes=VMEM_LIMIT
        ),
    )(source_field, mean_operator, field_operators, adjacency, mode_masks)
    return x, r


def solution(mesh):
    in_specs = (
        P("space", None, None, "mode"),
        P("space", None, None, None),
        P(None, "space", None, None, None),
        P("space", None, None),
        P(),
    )
    out_specs = (P("space", None, None, "mode"), P("space", None, None, "mode"))
    return jax.shard_map(
        functools.partial(per_device, mesh.shape["mode"], mesh.shape["space"]),
        mesh=mesh, in_specs=in_specs, out_specs=out_specs, check_vma=False,
    )
```

```python
import functools

import jax
import jax.numpy as jnp
from jax import lax
from jax.experimental import pallas as pl
from jax.experimental.pallas import tpu as pltpu
from jax.sharding import PartitionSpec as P

DEGREE = 4
COUPLING = 0.5773502691896258
THETA = 1.0
DELTA = 0.7
CHUNKS = 4
GROUP = 2
LAG = 4
LEAD = 3
SLOTS = 4
SECOND = 5
ORDER = ((-1, 0), (-1, 1), (0, 0), (0, 1), (1, 0), (1, 1), (2, 0), (-1, 2), (2, 1), (0, 2), (3, 0), (-1, 3), (1, 2), (3, 1), (0, 3), (2, 2), (1, 3), (3, 2), (2, 3), (3, 3))
RELAYED_GROUP = 1
VMEM_LIMIT = 56_000_000
MESH = pl.DeviceIdType.MESH


def prepare(raw, e, slot, modes_dev, adj_ref, mask_ref, w_hi, w_lo):
    face, blk = w_hi.shape[1], raw.shape[2]
    layer, f = e // face, lax.rem(e, face)
    for op in range(w_hi.shape[3] // blk):
        if op == 0:
            weights = [None]
        else:
            weights = [
                jnp.where(mask_ref[j] == modes_dev * (1 << (op - 1)), COUPLING, 0.0).astype(jnp.float32)
                for j in range(raw.shape[1] - 1)
            ]

        def block(s):
            lanes = slice(s * blk, (s + 1) * blk)
            if op == 0:
                return raw[slot, 0, :, lanes]
            total = weights[0] * raw[slot, 1, :, lanes]
            for j in range(1, len(weights)):
                total = total + weights[j] * raw[slot, 1 + j, :, lanes]
            return total

        own = block(0)
        sides = [block(3 + s) for s in range(adj_ref.shape[2])]
        parts = []
        for g in range(face):
            total = jnp.where(f == g, 1.0, 0.0).astype(jnp.float32) * own
            for s, side in enumerate(sides):
                total = total + jnp.where(adj_ref[layer, f, s] == g, 1.0, 0.0).astype(jnp.float32) * side
            parts.append(total)
        parts += [block(1), block(2)]
        for at, part in enumerate(parts):
            part = part.T
            high = part.astype(jnp.bfloat16)
            low = (part - high.astype(jnp.float32)).astype(jnp.bfloat16)
            w_hi[layer, f, at * blk : (at + 1) * blk, op * blk : (op + 1) * blk] = high
            w_lo[layer, f, at * blk : (at + 1) * blk, op * blk : (op + 1) * blk] = low


def schedule(chunks):
    group = min(GROUP, chunks)
    items = list(ORDER) if chunks == CHUNKS else []
    if not items:
        items = [(-1, c) for c in range(chunks)]
        for turn in range(DEGREE + LAG * (chunks // group - 1)):
            for c in range(chunks):
                t = turn - LAG * (c // group)
                if 0 <= t < DEGREE:
                    items.append((t, c))
    assert sorted(items) == [(t, c) for t in range(-1, DEGREE) for c in range(chunks)]
    plan, told = [], set()
    for at, item in enumerate(items):
        ahead = [step for step in items[at + 1 :] if step[0] >= 0][:1]
        if ahead and (ahead[0] in told or (ahead[0][0] - 1, ahead[0][1]) not in items[: at + 1]):
            ahead = []
        plan.append(item + (ahead[0] if ahead else (-1, 0)))
        told.update(ahead)
    assert told == {item for item in items if item[0] >= 0}
    return plan


def solve_kernel(
    peers, spaces, chunks, modes_dev, source, mean, fields, adj, masks, x_out, r_out,
    raw, w_hi, w_lo, direction, res, x, split, acc, halo_low, halo_up, relay, stage, src, x_land, r_land,
    w_sem, stage_sem, own_sem, in_send, in_recv, low_send, low_recv, up_send, up_recv,
    relay_send, relay_recv, forward_send, forward_recv, out_send, out_recv, own_out,
):
    layers, face, inner, width = w_hi.shape
    blk = inner // (face + 2)
    bits = peers.bit_length() - 1
    rows = direction.shape[4]
    lc = rows // peers
    me = lax.axis_index("mode")
    s = lax.axis_index("space")
    has_low = s > 0
    has_up = s < spaces - 1
    relayed = spaces >= 4 and spaces % 2 == 0 and face % 2 == 0
    groups = 2 if face % 2 == 0 else 1
    per = face // groups
    odd = lax.rem(s, 2) == 1
    even = jnp.logical_not(odd)
    both = jnp.logical_and
    elements = layers * face

    def loads(e):
        slot = lax.rem(e, SLOTS)
        l, f = e // face, lax.rem(e, face)
        return (
            pltpu.make_async_copy(mean.at[l, f], raw.at[slot, 0], w_sem.at[slot, 0]),
            pltpu.make_async_copy(fields.at[:, l, f], raw.at[slot, pl.ds(1, fields.shape[0])], w_sem.at[slot, 1]),
        )

    bands = min(chunks, max(modes_dev // 128, 1))
    band = modes_dev // bands
    in_band = chunks // bands

    def fetch(n):
        modes = pl.ds(n * band, band)
        return pltpu.make_async_copy(source.at[:, :, :, modes], stage.at[:, :, :, modes], stage_sem.at[n])

    def turn(n):
        fetch(n).wait()
        modes = slice(n * band, (n + 1) * band)
        for l in range(layers):
            for f in range(face):
                src[l, f, modes] = stage[l, f, :, modes].T * (1.0 / THETA)

    for n in range(bands):
        fetch(n).start()
    for e in range(min(SLOTS, elements)):
        for load in loads(e):
            load.start()

    barrier = pltpu.get_barrier_semaphore()
    for k in range(1, peers):
        pl.semaphore_signal(barrier, inc=1, device_id={"mode": lax.rem(me + k, peers)}, device_id_type=MESH)

    @pl.when(has_low)
    def _():
        pl.semaphore_signal(barrier, inc=1, device_id={"space": s - 1}, device_id_type=MESH)

    @pl.when(has_up)
    def _():
        pl.semaphore_signal(barrier, inc=1, device_id={"space": s + 1}, device_id_type=MESH)

    expected = peers - 1 + has_low.astype(jnp.int32) + has_up.astype(jnp.int32)
    if relayed:
        far_low, far_up = s >= 2, s < spaces - 2
        expected = expected + far_low.astype(jnp.int32) + far_up.astype(jnp.int32)

        @pl.when(far_low)
        def _():
            pl.semaphore_signal(barrier, inc=1, device_id={"space": s - 2}, device_id_type=MESH)

        @pl.when(far_up)
        def _():
            pl.semaphore_signal(barrier, inc=1, device_id={"space": s + 2}, device_id_type=MESH)

    turn(0)
    with jax.named_scope('barrier'):
        pl.semaphore_wait(barrier, expected)

    def slab(ref, c, h, part=slice(None)):
        return ref.at[c, :, part, pl.ds(pl.multiple_of(h * lc, lc), lc), :]

    def piece(ref, c, h, part=slice(None)):
        return ref.at[:, part, pl.ds(pl.multiple_of((c * peers + h) * lc, lc), lc), :]

    hops = sorted(range(1, peers), key=lambda k: abs(k - peers // 2))

    def in_start(c):
        for g in reversed(range(groups)) if RELAYED_GROUP else range(groups):
            part = pl.ds(g * per, per)
            for k in hops:
                to = lax.rem(me + k, peers)
                pltpu.make_async_remote_copy(
                    src_ref=piece(src, c, to, part), dst_ref=slab(direction.at[0], c, me, part),
                    send_sem=in_send.at[0], recv_sem=in_recv.at[c, g],
                    device_id={"mode": to}, device_id_type=MESH,
                ).start()
        own_copy(c).start()

    def whole(ref, count, send_sem, recv_sem, faces=face):
        part = ref.at[:, pl.ds(0, faces), pl.ds(0, count), :]
        return pltpu.make_async_remote_copy(
            src_ref=part, dst_ref=part, send_sem=send_sem, recv_sem=recv_sem,
            device_id={"mode": lax.rem(me + 1, peers)}, device_id_type=MESH,
        )

    def own_copy(c):
        return pltpu.make_async_copy(piece(src, c, me), slab(direction.at[0], c, me), own_sem.at[c])

    def to_low(t, c, g):
        part = pl.ds(g * per, per)
        return pltpu.make_async_remote_copy(
            src_ref=direction.at[lax.rem(t, 2), c, 0, part], dst_ref=halo_up.at[t, c, part],
            send_sem=low_send.at[lax.rem(t, 2), c, g], recv_sem=up_recv.at[lax.rem(t, 2), c, g],
            device_id={"space": s - 1}, device_id_type=MESH,
        )

    def to_up(t, c, g):
        part = pl.ds(g * per, per)
        return pltpu.make_async_remote_copy(
            src_ref=direction.at[lax.rem(t, 2), c, layers - 1, part], dst_ref=halo_low.at[t, c, part],
            send_sem=up_send.at[lax.rem(t, 2), c, g], recv_sem=low_recv.at[lax.rem(t, 2), c, g],
            device_id={"space": s + 1}, device_id_type=MESH,
        )

    def to_relay(t, c, layer, offset):
        return pltpu.make_async_remote_copy(
            src_ref=direction.at[lax.rem(t, 2), c, layer, pl.ds(RELAYED_GROUP * per, per)], dst_ref=relay.at[t, c],
            send_sem=relay_send.at[lax.rem(t, 2), c], recv_sem=relay_recv.at[lax.rem(t, 2), c],
            device_id={"space": s + offset}, device_id_type=MESH,
        )

    def forward(t, c, halo, offset):
        return pltpu.make_async_remote_copy(
            src_ref=relay.at[t, c], dst_ref=halo.at[t, c, pl.ds(RELAYED_GROUP * per, per)],
            send_sem=forward_send.at[0], recv_sem=forward_recv.at[lax.rem(t, 2), c],
            device_id={"space": s + offset}, device_id_type=MESH,
        )

    def halo_each(t, c, g, act):
        hop = relayed and g == RELAYED_GROUP

        @pl.when(both(even, has_low))
        def _():
            act(to_relay(t, c, 0, -2) if hop else to_low(t, c, g))

        @pl.when(both(odd, has_up))
        def _():
            act(to_relay(t, c, layers - 1, 2) if hop else to_up(t, c, g))

        @pl.when(both(odd, has_low))
        def _():
            act(to_low(t, c, g))

        @pl.when(both(even, has_up))
        def _():
            act(to_up(t, c, g))

    def halo_start(t, c, g):
        halo_each(t, c, g, lambda copy: copy.start())

    def halo_sent(t, c):
        for g in range(groups):
            halo_each(t, c, g, lambda copy: copy.wait_send())

    def forward_each(t, c, act):
        if relayed:

            @pl.when(both(odd, s >= 3))
            def _():
                act(forward(t, c, halo_low, -1))

            @pl.when(both(even, s < spaces - 3))
            def _():
                act(forward(t, c, halo_up, 1))

    def halo_forward(t, c):
        if relayed:

            @pl.when(jnp.logical_or(both(odd, s >= 3), both(even, s < spaces - 3)))
            def _():
                to_relay(t, c, 0, jnp.where(odd, -1, 1)).wait_recv()

            forward_each(t, c, lambda copy: copy.start())

    def halo_arrived(t, c, g):
        hop = relayed and g == RELAYED_GROUP

        @pl.when(both(odd, has_low))
        def _():
            to_up(t, c, g).wait_recv()

        @pl.when(both(even, has_up))
        def _():
            to_low(t, c, g).wait_recv()

        @pl.when(both(even, has_low))
        def _():
            (forward(t, c, halo_low, -1) if hop else to_up(t, c, g)).wait_recv()

        @pl.when(both(odd, has_up))
        def _():
            (forward(t, c, halo_up, 1) if hop else to_low(t, c, g)).wait_recv()

    def out_start(which, ref, land, c):
        for k in hops:
            to = lax.rem(me + k, peers)
            pltpu.make_async_remote_copy(
                src_ref=slab(ref, c, to), dst_ref=piece(land, c, me),
                send_sem=out_send.at[which], recv_sem=out_recv.at[which, c // in_band],
                device_id={"mode": to}, device_id_type=MESH,
            ).start()
        pltpu.make_async_copy(slab(ref, c, me), piece(land, c, me), own_out.at[which, c // in_band]).start()

    def out_finish(which, land, out, n):
        count = in_band * (peers - 1) * lc
        whole(land, count, out_send.at[which], out_recv.at[which, n]).wait_recv()
        own = land.at[:, :, pl.ds(0, in_band * lc), :]
        pltpu.make_async_copy(own, own, own_out.at[which, n]).wait()
        modes = slice(n * band, (n + 1) * band)
        for l in range(layers):
            for f in range(face):
                out[l, f, :, modes] = land[l, f, modes].T

    in_start(0)
    for n in range(1, bands):
        turn(n)

    @pl.when(jnp.logical_not(has_low))
    def _():
        halo_low[...] = jnp.zeros_like(halo_low)

    @pl.when(jnp.logical_not(has_up))
    def _():
        halo_up[...] = jnp.zeros_like(halo_up)

    def land(c):
        own_copy(c).wait()
        for g in reversed(range(groups)) if RELAYED_GROUP else range(groups):
            whole(src, (peers - 1) * lc, in_send.at[0], in_recv.at[c, g], per).wait_recv()
            halo_start(0, c, g)

        @pl.when(c == min(1, chunks - 1))
        def _():
            for late in range(2, chunks):
                in_start(late)

    items = schedule(chunks)

    def build(e, carry):
        for load in loads(e):
            load.wait()
        prepare(raw, e, lax.rem(e, SLOTS), modes_dev, adj, masks, w_hi, w_lo)

        @pl.when(e + SLOTS < elements)
        def _():
            for load in loads(e + SLOTS):
                load.start()

        if chunks > 1:

            @pl.when(e == SECOND)
            def _():
                in_start(1)

        return carry

    with jax.named_scope('build'):
        lax.fori_loop(0, elements, build, 0)

    def halves(value):
        high = value.astype(jnp.bfloat16)
        return high, (value - high.astype(jnp.float32)).astype(jnp.bfloat16)

    def product(a, l, f, lo, hi):
        def dot(left, right):
            return lax.dot_general(left, right, (((1,), (0,)), ((), ())), preferred_element_type=jnp.float32)

        y = dot(a, w_hi[l, f, lo:hi])
        return y[:rows] + y[rows:] + dot(a[:rows], w_lo[l, f, lo:hi])

    def keep_split(c, l, f, value):
        high, low = halves(value)
        split[c, l, :rows, f * blk : (f + 1) * blk] = high
        split[c, l, rows:, f * blk : (f + 1) * blk] = low

    sigma = THETA / DELTA
    last = (DEGREE - 1) % 2
    ratios = [1.0 / sigma]
    for _ in range(DEGREE):
        ratios.append(1.0 / (2.0 * sigma - ratios[-1]))

    def item(i):
        found = [jnp.int32(-1)] * 4
        for at, entry in enumerate(items):
            found = [jnp.where(i == at, value, old) for value, old in zip(entry, found)]
        return found

    def side(c, l, f, halo, t):
        if 0 <= l < layers:
            return split[c, l, :, f * blk : (f + 1) * blk]
        return jnp.concatenate(halves(halo[t, c, f]), axis=0)

    def advance(i, carry):
        t, c, t_next, c_next = item(i)

        @pl.when(t < 0)
        def _():
            with jax.named_scope('land'):
                land(c)

            for l in range(layers):
                for f in range(face):
                    d = direction[0, c, l, f]
                    res[c, l, f] = d
                    x[0, c, l, f] = d
                    keep_split(c, l, f, d)

        now = lax.rem(t + 2, 2)
        keep, add = jnp.float32(0.0), jnp.float32(0.0)
        for at in range(DEGREE - 1):
            keep = jnp.where(t == at, jnp.float32(ratios[at + 1] * ratios[at]), keep)
            add = jnp.where(t == at, jnp.float32(2.0 * ratios[at + 1] / DELTA), add)

        for g in range(groups):

            @pl.when(t >= 0)
            def _():
                with jax.named_scope(f'wait{g}'):
                    halo_arrived(t, c, g)

                if g == 0:

                    @pl.when(t > 0)
                    def _():
                        halo_sent(t - 1, c)

                for f in range(g * per, (g + 1) * per):
                    ys = []
                    for l in range(layers):
                        a = jnp.concatenate([side(c, l - 1, f, halo_low, t), side(c, l + 1, f, halo_up, t)], axis=1)
                        ys.append(acc[c, l, f] + product(a, l, f, face * blk, inner))
                    for l, y in enumerate(ys):
                        d = direction[now, c, l, f]
                        total = d + y[:, :blk]
                        for b in range(bits):
                            term = y[:, (b + 1) * blk : (b + 2) * blk]
                            total = total + jnp.concatenate(
                                [term[(h ^ (1 << b)) * lc : ((h ^ (1 << b)) + 1) * lc] for h in range(peers)], axis=0
                            )
                        r = res[c, l, f] - total
                        res[c, l, f] = r
                        d_new = keep * d + add * r
                        direction[1 - now, c, l, f] = d_new
                        x[1 - now, c, l, f] = x[now, c, l, f] + d_new
                        keep_split(c, l, f, d_new)

                @pl.when(t < DEGREE - 1)
                def _():
                    halo_start(t + 1, c, g)

        @pl.when(t == DEGREE - 2)
        def _():
            out_start(0, x.at[last], x_land, c)

        @pl.when(t == DEGREE - 1)
        def _():
            out_start(1, res, r_land, c)

        @pl.when(t < DEGREE - 1)
        def _():
            for l in range(layers):
                a = split[c, l]
                for f in range(face):
                    acc[c, l, f] = product(a, l, f, 0, face * blk)

        @pl.when(t_next >= 0)
        def _():
            with jax.named_scope('fwd'):
                halo_forward(t_next, c_next)

        return carry

    lax.fori_loop(0, len(items), advance, 0)

    with jax.named_scope('sent'):
        for c in range(chunks):
            halo_sent(DEGREE - 1, c)
        everything = (peers - 1) * chunks * lc
        whole(src, everything, in_send.at[0], in_recv.at[0, 0]).wait_send()
        if relayed:

            @pl.when(jnp.logical_or(both(odd, s >= 3), both(even, s < spaces - 3)))
            def _():
                pltpu.make_async_remote_copy(
                    src_ref=relay, dst_ref=relay, send_sem=forward_send.at[0], recv_sem=forward_recv.at[0, 0],
                    device_id={"space": s + jnp.where(odd, -1, 1)}, device_id_type=MESH,
                ).wait_send()

    for n in range(bands):
        with jax.named_scope(f'finx{n}'):
            out_finish(0, x_land, x_out, n)
        with jax.named_scope(f'finr{n}'):
            out_finish(1, r_land, r_out, n)
    with jax.named_scope('end'):
        for which, land, out in ((0, x_land, x_out), (1, r_land, r_out)):
            whole(land, everything, out_send.at[which], out_recv.at[which, 0]).wait_send()


def deliver(x, r, x_out, r_out, sem):
    copies = [pltpu.make_async_copy(x, x_out, sem.at[0]), pltpu.make_async_copy(r, r_out, sem.at[1])]
    for copy in copies:
        copy.start()
    for copy in copies:
        copy.wait()


def per_device(peers, spaces, source_field, mean_operator, field_operators, adjacency, mode_masks):
    layers, face, blk, modes_dev = source_field.shape
    bits = peers.bit_length() - 1
    chunks = CHUNKS
    while modes_dev % (peers * chunks * 8):
        chunks //= 2
    rows = modes_dev // chunks
    groups = 2 if face % 2 == 0 else 1
    weights = pltpu.VMEM((layers, face, (face + 2) * blk, (bits + 1) * blk), jnp.bfloat16)
    out = pltpu.VMEM(source_field.shape, jnp.float32)
    landing = pltpu.VMEM((layers, face, modes_dev, blk), jnp.float32)
    bands = min(chunks, max(modes_dev // 128, 1))
    field = (chunks, layers, face, rows, blk)
    halo = pltpu.VMEM((DEGREE, chunks, face, rows, blk), jnp.float32)
    dma = pltpu.SemaphoreType.DMA
    x, r = pl.pallas_call(
        functools.partial(solve_kernel, peers, spaces, chunks, modes_dev),
        in_specs=[
            pl.BlockSpec(memory_space=pl.ANY),
            pl.BlockSpec(memory_space=pl.ANY),
            pl.BlockSpec(memory_space=pl.ANY),
            pl.BlockSpec(memory_space=pltpu.SMEM),
            pl.BlockSpec(memory_space=pltpu.SMEM),
        ],
        out_specs=(pl.BlockSpec(memory_space=pltpu.VMEM), pl.BlockSpec(memory_space=pltpu.VMEM)),
        out_shape=(out, out),
        scratch_shapes=[
            pltpu.VMEM((SLOTS, 1 + field_operators.shape[0]) + mean_operator.shape[2:], jnp.float32),
            weights,
            weights,
            pltpu.VMEM((2,) + field, jnp.float32),
            pltpu.VMEM(field, jnp.float32),
            pltpu.VMEM((2,) + field, jnp.float32),
            pltpu.VMEM((chunks, layers, 2 * rows, face * blk), jnp.bfloat16),
            pltpu.VMEM((chunks, layers, face, rows, (bits + 1) * blk), jnp.float32),
            halo,
            halo,
            pltpu.VMEM((DEGREE, chunks, face // groups, rows, blk), jnp.float32),
            pltpu.VMEM(source_field.shape, jnp.float32),
            landing,
            landing,
            landing,
            dma((SLOTS, 2)),
            dma((bands,)),
            dma((chunks,)),
            dma((1,)),
            dma((chunks, groups)),
            dma((2, chunks, groups)),
            dma((2, chunks, groups)),
            dma((2, chunks, groups)),
            dma((2, chunks, groups)),
            dma((2, chunks)),
            dma((2, chunks)),
            dma((1,)),
            dma((2, chunks)),
            dma((2,)),
            dma((2, bands)),
            dma((2, bands)),
        ],
        compiler_params=pltpu.CompilerParams(
            collective_id=0, has_side_effects=True, vmem_limit_bytes=VMEM_LIMIT
        ),
    )(source_field, mean_operator, field_operators, adjacency, mode_masks)
    return x, r


def solution(mesh):
    in_specs = (
        P("space", None, None, "mode"),
        P("space", None, None, None),
        P(None, "space", None, None, None),
        P("space", None, None),
        P(),
    )
    out_specs = (P("space", None, None, "mode"), P("space", None, None, "mode"))
    return jax.shard_map(
        functools.partial(per_device, mesh.shape["mode"], mesh.shape["space"]),
        mesh=mesh, in_specs=in_specs, out_specs=out_specs, check_vma=False,
    )
```

```python
import functools

import jax
import jax.numpy as jnp
from jax import lax
from jax.experimental import pallas as pl
from jax.experimental.pallas import tpu as pltpu
from jax.sharding import PartitionSpec as P

DEGREE = 4
COUPLING = 0.5773502691896258
THETA = 1.0
DELTA = 0.7
CHUNKS = 4
GROUP = 2
LAG = 4
LEAD = 3
SLOTS = 4
SECOND = 5
EARLY = 0
ORDER = ((-1, 0), (-1, 1), (0, 0), (0, 1), (1, 0), (-1, 2), (1, 1), (2, 0), (0, 2), (2, 1), (3, 0), (-1, 3), (1, 2), (3, 1), (0, 3), (2, 2), (1, 3), (3, 2), (2, 3), (3, 3))
RELAYED_GROUP = 1
VMEM_LIMIT = 56_000_000
MESH = pl.DeviceIdType.MESH


def prepare(raw, e, slot, modes_dev, adj_ref, mask_ref, w_hi, w_lo):
    face, blk = w_hi.shape[1], raw.shape[2]
    layer, f = e // face, lax.rem(e, face)
    for op in range(w_hi.shape[3] // blk):
        if op == 0:
            weights = [None]
        else:
            weights = [
                jnp.where(mask_ref[j] == modes_dev * (1 << (op - 1)), COUPLING, 0.0).astype(jnp.float32)
                for j in range(raw.shape[1] - 1)
            ]

        def block(s):
            lanes = slice(s * blk, (s + 1) * blk)
            if op == 0:
                return raw[slot, 0, :, lanes]
            total = weights[0] * raw[slot, 1, :, lanes]
            for j in range(1, len(weights)):
                total = total + weights[j] * raw[slot, 1 + j, :, lanes]
            return total

        own = block(0)
        sides = [block(3 + s) for s in range(adj_ref.shape[2])]
        parts = []
        for g in range(face):
            total = jnp.where(f == g, 1.0, 0.0).astype(jnp.float32) * own
            for s, side in enumerate(sides):
                total = total + jnp.where(adj_ref[layer, f, s] == g, 1.0, 0.0).astype(jnp.float32) * side
            parts.append(total)
        parts += [block(1), block(2)]
        for at, part in enumerate(parts):
            part = part.T
            high = part.astype(jnp.bfloat16)
            low = (part - high.astype(jnp.float32)).astype(jnp.bfloat16)
            w_hi[layer, f, at * blk : (at + 1) * blk, op * blk : (op + 1) * blk] = high
            w_lo[layer, f, at * blk : (at + 1) * blk, op * blk : (op + 1) * blk] = low


def schedule(chunks):
    group = min(GROUP, chunks)
    items = list(ORDER) if chunks == CHUNKS else []
    if not items:
        items = [(-1, c) for c in range(chunks)]
        for turn in range(DEGREE + LAG * (chunks // group - 1)):
            for c in range(chunks):
                t = turn - LAG * (c // group)
                if 0 <= t < DEGREE:
                    items.append((t, c))
    assert sorted(items) == [(t, c) for t in range(-1, DEGREE) for c in range(chunks)]
    plan, told = [], set()
    for at, item in enumerate(items):
        ahead = [step for step in items[at + 1 :] if step[0] >= 0][:1]
        if ahead and (ahead[0] in told or (ahead[0][0] - 1, ahead[0][1]) not in items[: at + 1]):
            ahead = []
        plan.append(item + (ahead[0] if ahead else (-1, 0)))
        told.update(ahead)
    assert told == {item for item in items if item[0] >= 0}
    return plan


def solve_kernel(
    peers, spaces, chunks, modes_dev, source, mean, fields, adj, masks, x_out, r_out,
    raw, w_hi, w_lo, direction, res, x, split, acc, halo_low, halo_up, relay, stage, src, x_land, r_land,
    w_sem, stage_sem, own_sem, in_send, in_recv, low_send, low_recv, up_send, up_recv,
    relay_send, relay_recv, forward_send, forward_recv, out_send, out_recv, own_out,
):
    layers, face, inner, width = w_hi.shape
    blk = inner // (face + 2)
    bits = peers.bit_length() - 1
    rows = direction.shape[4]
    lc = rows // peers
    me = lax.axis_index("mode")
    s = lax.axis_index("space")
    has_low = s > 0
    has_up = s < spaces - 1
    relayed = spaces >= 4 and spaces % 2 == 0 and face % 2 == 0
    groups = 2 if face % 2 == 0 else 1
    per = face // groups
    odd = lax.rem(s, 2) == 1
    even = jnp.logical_not(odd)
    both = jnp.logical_and
    elements = layers * face

    def loads(e):
        slot = lax.rem(e, SLOTS)
        l, f = e // face, lax.rem(e, face)
        return (
            pltpu.make_async_copy(mean.at[l, f], raw.at[slot, 0], w_sem.at[slot, 0]),
            pltpu.make_async_copy(fields.at[:, l, f], raw.at[slot, pl.ds(1, fields.shape[0])], w_sem.at[slot, 1]),
        )

    bands = min(chunks, max(modes_dev // 128, 1))
    band = modes_dev // bands
    in_band = chunks // bands

    def fetch(n):
        modes = pl.ds(n * band, band)
        return pltpu.make_async_copy(source.at[:, :, :, modes], stage.at[:, :, :, modes], stage_sem.at[n])

    def turn(n):
        with jax.named_scope('fetch'):
            fetch(n).wait()
        modes = slice(n * band, (n + 1) * band)
        for l in range(layers):
            for f in range(face):
                src[l, f, modes] = stage[l, f, :, modes].T * (1.0 / THETA)

    for n in range(bands):
        fetch(n).start()

    barrier = pltpu.get_barrier_semaphore()
    for k in range(1, peers):
        pl.semaphore_signal(barrier, inc=1, device_id={"mode": lax.rem(me + k, peers)}, device_id_type=MESH)

    @pl.when(has_low)
    def _():
        pl.semaphore_signal(barrier, inc=1, device_id={"space": s - 1}, device_id_type=MESH)

    @pl.when(has_up)
    def _():
        pl.semaphore_signal(barrier, inc=1, device_id={"space": s + 1}, device_id_type=MESH)

    expected = peers - 1 + has_low.astype(jnp.int32) + has_up.astype(jnp.int32)
    if relayed:
        far_low, far_up = s >= 2, s < spaces - 2
        expected = expected + far_low.astype(jnp.int32) + far_up.astype(jnp.int32)

        @pl.when(far_low)
        def _():
            pl.semaphore_signal(barrier, inc=1, device_id={"space": s - 2}, device_id_type=MESH)

        @pl.when(far_up)
        def _():
            pl.semaphore_signal(barrier, inc=1, device_id={"space": s + 2}, device_id_type=MESH)

    turn(0)
    for e in range(min(SLOTS, elements)):
        for load in loads(e):
            load.start()
    with jax.named_scope('barrier'):
        pl.semaphore_wait(barrier, expected)

    def slab(ref, c, h, part=slice(None)):
        return ref.at[c, :, part, pl.ds(pl.multiple_of(h * lc, lc), lc), :]

    def piece(ref, c, h, part=slice(None)):
        return ref.at[:, part, pl.ds(pl.multiple_of((c * peers + h) * lc, lc), lc), :]

    hops = sorted(range(1, peers), key=lambda k: abs(k - peers // 2))

    def in_start(c):
        for g in reversed(range(groups)) if RELAYED_GROUP else range(groups):
            part = pl.ds(g * per, per)
            for k in hops:
                to = lax.rem(me + k, peers)
                pltpu.make_async_remote_copy(
                    src_ref=piece(src, c, to, part), dst_ref=slab(direction.at[0], c, me, part),
                    send_sem=in_send.at[0], recv_sem=in_recv.at[c, g],
                    device_id={"mode": to}, device_id_type=MESH,
                ).start()
        own_copy(c).start()

    def whole(ref, count, send_sem, recv_sem, faces=face):
        part = ref.at[:, pl.ds(0, faces), pl.ds(0, count), :]
        return pltpu.make_async_remote_copy(
            src_ref=part, dst_ref=part, send_sem=send_sem, recv_sem=recv_sem,
            device_id={"mode": lax.rem(me + 1, peers)}, device_id_type=MESH,
        )

    def own_copy(c):
        return pltpu.make_async_copy(piece(src, c, me), slab(direction.at[0], c, me), own_sem.at[c])

    def to_low(t, c, g):
        part = pl.ds(g * per, per)
        return pltpu.make_async_remote_copy(
            src_ref=direction.at[lax.rem(t, 2), c, 0, part], dst_ref=halo_up.at[t, c, part],
            send_sem=low_send.at[lax.rem(t, 2), c, g], recv_sem=up_recv.at[lax.rem(t, 2), c, g],
            device_id={"space": s - 1}, device_id_type=MESH,
        )

    def to_up(t, c, g):
        part = pl.ds(g * per, per)
        return pltpu.make_async_remote_copy(
            src_ref=direction.at[lax.rem(t, 2), c, layers - 1, part], dst_ref=halo_low.at[t, c, part],
            send_sem=up_send.at[lax.rem(t, 2), c, g], recv_sem=low_recv.at[lax.rem(t, 2), c, g],
            device_id={"space": s + 1}, device_id_type=MESH,
        )

    def to_relay(t, c, layer, offset):
        return pltpu.make_async_remote_copy(
            src_ref=direction.at[lax.rem(t, 2), c, layer, pl.ds(RELAYED_GROUP * per, per)], dst_ref=relay.at[t, c],
            send_sem=relay_send.at[lax.rem(t, 2), c], recv_sem=relay_recv.at[lax.rem(t, 2), c],
            device_id={"space": s + offset}, device_id_type=MESH,
        )

    def forward(t, c, halo, offset):
        return pltpu.make_async_remote_copy(
            src_ref=relay.at[t, c], dst_ref=halo.at[t, c, pl.ds(RELAYED_GROUP * per, per)],
            send_sem=forward_send.at[0], recv_sem=forward_recv.at[lax.rem(t, 2), c],
            device_id={"space": s + offset}, device_id_type=MESH,
        )

    def halo_each(t, c, g, act):
        hop = relayed and g == RELAYED_GROUP

        @pl.when(both(even, has_low))
        def _():
            act(to_relay(t, c, 0, -2) if hop else to_low(t, c, g))

        @pl.when(both(odd, has_up))
        def _():
            act(to_relay(t, c, layers - 1, 2) if hop else to_up(t, c, g))

        @pl.when(both(odd, has_low))
        def _():
            act(to_low(t, c, g))

        @pl.when(both(even, has_up))
        def _():
            act(to_up(t, c, g))

    def halo_start(t, c, g):
        halo_each(t, c, g, lambda copy: copy.start())

    def halo_sent(t, c):
        for g in range(groups):
            halo_each(t, c, g, lambda copy: copy.wait_send())

    def forward_each(t, c, act):
        if relayed:

            @pl.when(both(odd, s >= 3))
            def _():
                act(forward(t, c, halo_low, -1))

            @pl.when(both(even, s < spaces - 3))
            def _():
                act(forward(t, c, halo_up, 1))

    def halo_forward(t, c):
        if relayed:

            @pl.when(jnp.logical_or(both(odd, s >= 3), both(even, s < spaces - 3)))
            def _():
                to_relay(t, c, 0, jnp.where(odd, -1, 1)).wait_recv()

            forward_each(t, c, lambda copy: copy.start())

    def halo_arrived(t, c, g):
        hop = relayed and g == RELAYED_GROUP

        @pl.when(both(odd, has_low))
        def _():
            to_up(t, c, g).wait_recv()

        @pl.when(both(even, has_up))
        def _():
            to_low(t, c, g).wait_recv()

        @pl.when(both(even, has_low))
        def _():
            (forward(t, c, halo_low, -1) if hop else to_up(t, c, g)).wait_recv()

        @pl.when(both(odd, has_up))
        def _():
            (forward(t, c, halo_up, 1) if hop else to_low(t, c, g)).wait_recv()

    def out_start(which, ref, land, c):
        for k in hops:
            to = lax.rem(me + k, peers)
            pltpu.make_async_remote_copy(
                src_ref=slab(ref, c, to), dst_ref=piece(land, c, me),
                send_sem=out_send.at[which], recv_sem=out_recv.at[which, c // in_band],
                device_id={"mode": to}, device_id_type=MESH,
            ).start()
        pltpu.make_async_copy(slab(ref, c, me), piece(land, c, me), own_out.at[which, c // in_band]).start()

    def out_finish(which, land, out, n):
        count = in_band * (peers - 1) * lc
        whole(land, count, out_send.at[which], out_recv.at[which, n]).wait_recv()
        own = land.at[:, :, pl.ds(0, in_band * lc), :]
        pltpu.make_async_copy(own, own, own_out.at[which, n]).wait()
        modes = slice(n * band, (n + 1) * band)
        for l in range(layers):
            for f in range(face):
                out[l, f, :, modes] = land[l, f, modes].T

    in_start(0)
    for n in range(1, bands):
        turn(n)

    @pl.when(jnp.logical_not(has_low))
    def _():
        halo_low[...] = jnp.zeros_like(halo_low)

    @pl.when(jnp.logical_not(has_up))
    def _():
        halo_up[...] = jnp.zeros_like(halo_up)

    turns = list(reversed(range(groups))) if RELAYED_GROUP else list(range(groups))

    def land(c, g):
        whole(src, (peers - 1) * lc, in_send.at[0], in_recv.at[c, g], per).wait_recv()
        halo_start(0, c, g)

    items = schedule(chunks)

    def build(e, carry):
        for load in loads(e):
            load.wait()
        prepare(raw, e, lax.rem(e, SLOTS), modes_dev, adj, masks, w_hi, w_lo)

        @pl.when(e + SLOTS < elements)
        def _():
            for load in loads(e + SLOTS):
                load.start()

        if chunks > 1:

            @pl.when(e == SECOND)
            def _():
                in_start(1)

        for place, g in enumerate(turns):

            @pl.when(e == elements - groups + place - EARLY)
            def _():
                if place == 0:
                    own_copy(0).wait()
                land(0, g)

        return carry

    with jax.named_scope('build'):
        lax.fori_loop(0, elements, build, 0)

    def halves(value):
        high = value.astype(jnp.bfloat16)
        return high, (value - high.astype(jnp.float32)).astype(jnp.bfloat16)

    def product(a, l, f, lo, hi):
        def dot(left, right):
            return lax.dot_general(left, right, (((1,), (0,)), ((), ())), preferred_element_type=jnp.float32)

        y = dot(a, w_hi[l, f, lo:hi])
        return y[:rows] + y[rows:] + dot(a[:rows], w_lo[l, f, lo:hi])

    def keep_split(c, l, f, value):
        high, low = halves(value)
        split[c, l, :rows, f * blk : (f + 1) * blk] = high
        split[c, l, rows:, f * blk : (f + 1) * blk] = low

    sigma = THETA / DELTA
    last = (DEGREE - 1) % 2
    ratios = [1.0 / sigma]
    for _ in range(DEGREE):
        ratios.append(1.0 / (2.0 * sigma - ratios[-1]))

    def item(i):
        found = [jnp.int32(-1)] * 4
        for at, entry in enumerate(items):
            found = [jnp.where(i == at, value, old) for value, old in zip(entry, found)]
        return found

    def side(c, l, f, halo, t):
        if 0 <= l < layers:
            return split[c, l, :, f * blk : (f + 1) * blk]
        return jnp.concatenate(halves(halo[t, c, f]), axis=0)

    def advance(i, carry):
        t, c, t_next, c_next = item(i)

        @pl.when(t < 0)
        def _():
            @pl.when(c > 0)
            def _():
                with jax.named_scope('land'):
                    own_copy(c).wait()
                    for g in turns:
                        land(c, g)

            @pl.when(c == min(1, chunks - 1))
            def _():
                for late in range(2, chunks):
                    in_start(late)

            for l in range(layers):
                for f in range(face):
                    d = direction[0, c, l, f]
                    res[c, l, f] = d
                    x[0, c, l, f] = d
                    keep_split(c, l, f, d)

        now = lax.rem(t + 2, 2)
        keep, add = jnp.float32(0.0), jnp.float32(0.0)
        for at in range(DEGREE - 1):
            keep = jnp.where(t == at, jnp.float32(ratios[at + 1] * ratios[at]), keep)
            add = jnp.where(t == at, jnp.float32(2.0 * ratios[at + 1] / DELTA), add)

        for g in range(groups):

            @pl.when(t >= 0)
            def _():
                with jax.named_scope(f'wait{g}'):
                    halo_arrived(t, c, g)

                if g == 0:

                    @pl.when(t > 0)
                    def _():
                        halo_sent(t - 1, c)

                for f in range(g * per, (g + 1) * per):
                    ys = []
                    for l in range(layers):
                        a = jnp.concatenate([side(c, l - 1, f, halo_low, t), side(c, l + 1, f, halo_up, t)], axis=1)
                        ys.append(acc[c, l, f] + product(a, l, f, face * blk, inner))
                    for l, y in enumerate(ys):
                        d = direction[now, c, l, f]
                        total = d + y[:, :blk]
                        for b in range(bits):
                            term = y[:, (b + 1) * blk : (b + 2) * blk]
                            total = total + jnp.concatenate(
                                [term[(h ^ (1 << b)) * lc : ((h ^ (1 << b)) + 1) * lc] for h in range(peers)], axis=0
                            )
                        r = res[c, l, f] - total
                        res[c, l, f] = r
                        d_new = keep * d + add * r
                        direction[1 - now, c, l, f] = d_new
                        x[1 - now, c, l, f] = x[now, c, l, f] + d_new
                        keep_split(c, l, f, d_new)

                @pl.when(t < DEGREE - 1)
                def _():
                    halo_start(t + 1, c, g)

        @pl.when(t == DEGREE - 2)
        def _():
            out_start(0, x.at[last], x_land, c)

        @pl.when(t == DEGREE - 1)
        def _():
            out_start(1, res, r_land, c)

        @pl.when(t < DEGREE - 1)
        def _():
            for l in range(layers):
                a = split[c, l]
                for f in range(face):
                    acc[c, l, f] = product(a, l, f, 0, face * blk)

        @pl.when(t_next >= 0)
        def _():
            with jax.named_scope('fwd'):
                halo_forward(t_next, c_next)

        return carry

    lax.fori_loop(0, len(items), advance, 0)

    with jax.named_scope('sent'):
        for c in range(chunks):
            halo_sent(DEGREE - 1, c)
        everything = (peers - 1) * chunks * lc
        whole(src, everything, in_send.at[0], in_recv.at[0, 0]).wait_send()
        if relayed:

            @pl.when(jnp.logical_or(both(odd, s >= 3), both(even, s < spaces - 3)))
            def _():
                pltpu.make_async_remote_copy(
                    src_ref=relay, dst_ref=relay, send_sem=forward_send.at[0], recv_sem=forward_recv.at[0, 0],
                    device_id={"space": s + jnp.where(odd, -1, 1)}, device_id_type=MESH,
                ).wait_send()

    for n in range(bands):
        with jax.named_scope(f'finx{n}'):
            out_finish(0, x_land, x_out, n)
        with jax.named_scope(f'finr{n}'):
            out_finish(1, r_land, r_out, n)
    with jax.named_scope('end'):
        for which, land, out in ((0, x_land, x_out), (1, r_land, r_out)):
            whole(land, everything, out_send.at[which], out_recv.at[which, 0]).wait_send()


def deliver(x, r, x_out, r_out, sem):
    copies = [pltpu.make_async_copy(x, x_out, sem.at[0]), pltpu.make_async_copy(r, r_out, sem.at[1])]
    for copy in copies:
        copy.start()
    for copy in copies:
        copy.wait()


def per_device(peers, spaces, source_field, mean_operator, field_operators, adjacency, mode_masks):
    layers, face, blk, modes_dev = source_field.shape
    bits = peers.bit_length() - 1
    chunks = CHUNKS
    while modes_dev % (peers * chunks * 8):
        chunks //= 2
    rows = modes_dev // chunks
    groups = 2 if face % 2 == 0 else 1
    weights = pltpu.VMEM((layers, face, (face + 2) * blk, (bits + 1) * blk), jnp.bfloat16)
    out = pltpu.VMEM(source_field.shape, jnp.float32)
    landing = pltpu.VMEM((layers, face, modes_dev, blk), jnp.float32)
    bands = min(chunks, max(modes_dev // 128, 1))
    field = (chunks, layers, face, rows, blk)
    halo = pltpu.VMEM((DEGREE, chunks, face, rows, blk), jnp.float32)
    dma = pltpu.SemaphoreType.DMA
    x, r = pl.pallas_call(
        functools.partial(solve_kernel, peers, spaces, chunks, modes_dev),
        in_specs=[
            pl.BlockSpec(memory_space=pl.ANY),
            pl.BlockSpec(memory_space=pl.ANY),
            pl.BlockSpec(memory_space=pl.ANY),
            pl.BlockSpec(memory_space=pltpu.SMEM),
            pl.BlockSpec(memory_space=pltpu.SMEM),
        ],
        out_specs=(pl.BlockSpec(memory_space=pltpu.VMEM), pl.BlockSpec(memory_space=pltpu.VMEM)),
        out_shape=(out, out),
        scratch_shapes=[
            pltpu.VMEM((SLOTS, 1 + field_operators.shape[0]) + mean_operator.shape[2:], jnp.float32),
            weights,
            weights,
            pltpu.VMEM((2,) + field, jnp.float32),
            pltpu.VMEM(field, jnp.float32),
            pltpu.VMEM((2,) + field, jnp.float32),
            pltpu.VMEM((chunks, layers, 2 * rows, face * blk), jnp.bfloat16),
            pltpu.VMEM((chunks, layers, face, rows, (bits + 1) * blk), jnp.float32),
            halo,
            halo,
            pltpu.VMEM((DEGREE, chunks, face // groups, rows, blk), jnp.float32),
            pltpu.VMEM(source_field.shape, jnp.float32),
            landing,
            landing,
            landing,
            dma((SLOTS, 2)),
            dma((bands,)),
            dma((chunks,)),
            dma((1,)),
            dma((chunks, groups)),
            dma((2, chunks, groups)),
            dma((2, chunks, groups)),
            dma((2, chunks, groups)),
            dma((2, chunks, groups)),
            dma((2, chunks)),
            dma((2, chunks)),
            dma((1,)),
            dma((2, chunks)),
            dma((2,)),
            dma((2, bands)),
            dma((2, bands)),
        ],
        compiler_params=pltpu.CompilerParams(
            collective_id=0, has_side_effects=True, vmem_limit_bytes=VMEM_LIMIT
        ),
    )(source_field, mean_operator, field_operators, adjacency, mode_masks)
    return x, r


def solution(mesh):
    in_specs = (
        P("space", None, None, "mode"),
        P("space", None, None, None),
        P(None, "space", None, None, None),
        P("space", None, None),
        P(),
    )
    out_specs = (P("space", None, None, "mode"), P("space", None, None, "mode"))
    return jax.shard_map(
        functools.partial(per_device, mesh.shape["mode"], mesh.shape["space"]),
        mesh=mesh, in_specs=in_specs, out_specs=out_specs, check_vma=False,
    )
```

```python
import functools

import jax
import jax.numpy as jnp
from jax import lax
from jax.experimental import pallas as pl
from jax.experimental.pallas import tpu as pltpu
from jax.sharding import PartitionSpec as P

DEGREE = 4
COUPLING = 0.5773502691896258
THETA = 1.0
DELTA = 0.7
CHUNKS = 4
GROUP = 2
LAG = 4
LEAD = 3
SLOTS = 4
SECOND = 5
EARLY = 0
ORDER = ((-1, 0), (-1, 1), (0, 0), (0, 1), (1, 0), (-1, 2), (1, 1), (2, 0), (0, 2), (2, 1), (3, 0), (-1, 3), (1, 2), (3, 1), (0, 3), (2, 2), (1, 3), (3, 2), (2, 3), (3, 3))
RELAYED_GROUP = 1
VMEM_LIMIT = 56_000_000
MESH = pl.DeviceIdType.MESH


def prepare(raw, e, slot, modes_dev, adj_ref, mask_ref, w_hi, w_lo):
    face, blk = w_hi.shape[1], raw.shape[2]
    layer, f = e // face, lax.rem(e, face)
    for op in range(w_hi.shape[3] // blk):
        if op == 0:
            weights = [None]
        else:
            weights = [
                jnp.where(mask_ref[j] == modes_dev * (1 << (op - 1)), COUPLING, 0.0).astype(jnp.float32)
                for j in range(raw.shape[1] - 1)
            ]

        def block(s):
            lanes = slice(s * blk, (s + 1) * blk)
            if op == 0:
                return raw[slot, 0, :, lanes]
            total = weights[0] * raw[slot, 1, :, lanes]
            for j in range(1, len(weights)):
                total = total + weights[j] * raw[slot, 1 + j, :, lanes]
            return total

        own = block(0)
        sides = [block(3 + s) for s in range(adj_ref.shape[2])]
        parts = []
        for g in range(face):
            total = jnp.where(f == g, 1.0, 0.0).astype(jnp.float32) * own
            for s, side in enumerate(sides):
                total = total + jnp.where(adj_ref[layer, f, s] == g, 1.0, 0.0).astype(jnp.float32) * side
            parts.append(total)
        parts += [block(1), block(2)]
        for at, part in enumerate(parts):
            part = part.T
            high = part.astype(jnp.bfloat16)
            low = (part - high.astype(jnp.float32)).astype(jnp.bfloat16)
            w_hi[layer, f, at * blk : (at + 1) * blk, op * blk : (op + 1) * blk] = high
            w_lo[layer, f, at * blk : (at + 1) * blk, op * blk : (op + 1) * blk] = low


def schedule(chunks):
    group = min(GROUP, chunks)
    items = list(ORDER) if chunks == CHUNKS else []
    if not items:
        items = [(-1, c) for c in range(chunks)]
        for turn in range(DEGREE + LAG * (chunks // group - 1)):
            for c in range(chunks):
                t = turn - LAG * (c // group)
                if 0 <= t < DEGREE:
                    items.append((t, c))
    assert sorted(items) == [(t, c) for t in range(-1, DEGREE) for c in range(chunks)]
    plan, told = [], set()
    for at, item in enumerate(items):
        ahead = [step for step in items[at + 1 :] if step[0] >= 0][:1]
        if ahead and (ahead[0] in told or (ahead[0][0] - 1, ahead[0][1]) not in items[: at + 1]):
            ahead = []
        plan.append(item + (ahead[0] if ahead else (-1, 0)))
        told.update(ahead)
    assert told == {item for item in items if item[0] >= 0}
    return plan


def solve_kernel(
    peers, spaces, chunks, modes_dev, source, mean, fields, adj, masks, x_out, r_out,
    raw, w_hi, w_lo, direction, res, x, split, acc, halo_low, halo_up, relay, stage, src, x_land, r_land,
    w_sem, stage_sem, own_sem, in_send, in_recv, low_send, low_recv, up_send, up_recv,
    relay_send, relay_recv, forward_send, forward_recv, out_send, out_recv, own_out,
):
    layers, face, inner, width = w_hi.shape
    blk = inner // (face + 2)
    bits = peers.bit_length() - 1
    rows = direction.shape[4]
    lc = rows // peers
    me = lax.axis_index("mode")
    s = lax.axis_index("space")
    has_low = s > 0
    has_up = s < spaces - 1
    relayed = spaces >= 4 and spaces % 2 == 0 and face % 2 == 0
    groups = 2 if face % 2 == 0 else 1
    per = face // groups
    odd = lax.rem(s, 2) == 1
    even = jnp.logical_not(odd)
    both = jnp.logical_and
    elements = layers * face

    def loads(e):
        slot = lax.rem(e, SLOTS)
        l, f = e // face, lax.rem(e, face)
        return (
            pltpu.make_async_copy(mean.at[l, f], raw.at[slot, 0], w_sem.at[slot, 0]),
            pltpu.make_async_copy(fields.at[:, l, f], raw.at[slot, pl.ds(1, fields.shape[0])], w_sem.at[slot, 1]),
        )

    bands = min(chunks, max(modes_dev // 128, 1))
    band = modes_dev // bands
    in_band = chunks // bands

    def fetch(n):
        modes = pl.ds(n * band, band)
        return pltpu.make_async_copy(source.at[:, :, :, modes], stage.at[:, :, :, modes], stage_sem.at[n])

    def turn(n):
        with jax.named_scope('fetch'):
            fetch(n).wait()
        modes = slice(n * band, (n + 1) * band)
        for l in range(layers):
            for f in range(face):
                src[l, f, modes] = stage[l, f, :, modes].T * (1.0 / THETA)

    for n in range(bands):
        fetch(n).start()

    barrier = pltpu.get_barrier_semaphore()
    for k in range(1, peers):
        pl.semaphore_signal(barrier, inc=1, device_id={"mode": lax.rem(me + k, peers)}, device_id_type=MESH)

    @pl.when(has_low)
    def _():
        pl.semaphore_signal(barrier, inc=1, device_id={"space": s - 1}, device_id_type=MESH)

    @pl.when(has_up)
    def _():
        pl.semaphore_signal(barrier, inc=1, device_id={"space": s + 1}, device_id_type=MESH)

    expected = peers - 1 + has_low.astype(jnp.int32) + has_up.astype(jnp.int32)
    if relayed:
        far_low, far_up = s >= 2, s < spaces - 2
        expected = expected + far_low.astype(jnp.int32) + far_up.astype(jnp.int32)

        @pl.when(far_low)
        def _():
            pl.semaphore_signal(barrier, inc=1, device_id={"space": s - 2}, device_id_type=MESH)

        @pl.when(far_up)
        def _():
            pl.semaphore_signal(barrier, inc=1, device_id={"space": s + 2}, device_id_type=MESH)

    turn(0)
    for e in range(min(SLOTS, elements)):
        for load in loads(e):
            load.start()
    with jax.named_scope('barrier'):
        pl.semaphore_wait(barrier, expected)

    def slab(ref, c, h, part=slice(None)):
        return ref.at[c, :, part, pl.ds(pl.multiple_of(h * lc, lc), lc), :]

    def piece(ref, c, h, part=slice(None)):
        return ref.at[:, part, pl.ds(pl.multiple_of((c * peers + h) * lc, lc), lc), :]

    hops = sorted(range(1, peers), key=lambda k: abs(k - peers // 2))

    def in_start(c):
        for g in reversed(range(groups)) if RELAYED_GROUP else range(groups):
            part = pl.ds(g * per, per)
            for k in hops:
                to = lax.rem(me + k, peers)
                pltpu.make_async_remote_copy(
                    src_ref=piece(src, c, to, part), dst_ref=slab(direction.at[0], c, me, part),
                    send_sem=in_send.at[0], recv_sem=in_recv.at[c, g],
                    device_id={"mode": to}, device_id_type=MESH,
                ).start()
        own_copy(c).start()

    def whole(ref, count, send_sem, recv_sem, faces=face):
        part = ref.at[:, pl.ds(0, faces), pl.ds(0, count), :]
        return pltpu.make_async_remote_copy(
            src_ref=part, dst_ref=part, send_sem=send_sem, recv_sem=recv_sem,
            device_id={"mode": lax.rem(me + 1, peers)}, device_id_type=MESH,
        )

    def own_copy(c):
        return pltpu.make_async_copy(piece(src, c, me), slab(direction.at[0], c, me), own_sem.at[c])

    def to_low(t, c, g):
        part = pl.ds(g * per, per)
        return pltpu.make_async_remote_copy(
            src_ref=direction.at[lax.rem(t, 2), c, 0, part], dst_ref=halo_up.at[t, c, part],
            send_sem=low_send.at[lax.rem(t, 2), c, g], recv_sem=up_recv.at[lax.rem(t, 2), c, g],
            device_id={"space": s - 1}, device_id_type=MESH,
        )

    def to_up(t, c, g):
        part = pl.ds(g * per, per)
        return pltpu.make_async_remote_copy(
            src_ref=direction.at[lax.rem(t, 2), c, layers - 1, part], dst_ref=halo_low.at[t, c, part],
            send_sem=up_send.at[lax.rem(t, 2), c, g], recv_sem=low_recv.at[lax.rem(t, 2), c, g],
            device_id={"space": s + 1}, device_id_type=MESH,
        )

    def to_relay(t, c, layer, offset):
        return pltpu.make_async_remote_copy(
            src_ref=direction.at[lax.rem(t, 2), c, layer, pl.ds(RELAYED_GROUP * per, per)], dst_ref=relay.at[t, c],
            send_sem=relay_send.at[lax.rem(t, 2), c], recv_sem=relay_recv.at[lax.rem(t, 2), c],
            device_id={"space": s + offset}, device_id_type=MESH,
        )

    def forward(t, c, halo, offset):
        return pltpu.make_async_remote_copy(
            src_ref=relay.at[t, c], dst_ref=halo.at[t, c, pl.ds(RELAYED_GROUP * per, per)],
            send_sem=forward_send.at[0], recv_sem=forward_recv.at[lax.rem(t, 2), c],
            device_id={"space": s + offset}, device_id_type=MESH,
        )

    def halo_each(t, c, g, act):
        hop = relayed and g == RELAYED_GROUP

        @pl.when(both(even, has_low))
        def _():
            act(to_relay(t, c, 0, -2) if hop else to_low(t, c, g))

        @pl.when(both(odd, has_up))
        def _():
            act(to_relay(t, c, layers - 1, 2) if hop else to_up(t, c, g))

        @pl.when(both(odd, has_low))
        def _():
            act(to_low(t, c, g))

        @pl.when(both(even, has_up))
        def _():
            act(to_up(t, c, g))

    def halo_start(t, c, g):
        halo_each(t, c, g, lambda copy: copy.start())

    def halo_sent(t, c):
        for g in range(groups):
            halo_each(t, c, g, lambda copy: copy.wait_send())

    def forward_each(t, c, act):
        if relayed:

            @pl.when(both(odd, s >= 3))
            def _():
                act(forward(t, c, halo_low, -1))

            @pl.when(both(even, s < spaces - 3))
            def _():
                act(forward(t, c, halo_up, 1))

    def halo_forward(t, c):
        if relayed:

            @pl.when(jnp.logical_or(both(odd, s >= 3), both(even, s < spaces - 3)))
            def _():
                to_relay(t, c, 0, jnp.where(odd, -1, 1)).wait_recv()

            forward_each(t, c, lambda copy: copy.start())

    def halo_arrived(t, c, g):
        hop = relayed and g == RELAYED_GROUP

        @pl.when(both(odd, has_low))
        def _():
            to_up(t, c, g).wait_recv()

        @pl.when(both(even, has_up))
        def _():
            to_low(t, c, g).wait_recv()

        @pl.when(both(even, has_low))
        def _():
            (forward(t, c, halo_low, -1) if hop else to_up(t, c, g)).wait_recv()

        @pl.when(both(odd, has_up))
        def _():
            (forward(t, c, halo_up, 1) if hop else to_low(t, c, g)).wait_recv()

    def out_start(which, ref, land, c, part=slice(None)):
        for k in hops:
            to = lax.rem(me + k, peers)
            pltpu.make_async_remote_copy(
                src_ref=slab(ref, c, to, part), dst_ref=piece(land, c, me, part),
                send_sem=out_send.at[which], recv_sem=out_recv.at[which, c // in_band],
                device_id={"mode": to}, device_id_type=MESH,
            ).start()
        pltpu.make_async_copy(slab(ref, c, me, part), piece(land, c, me, part), own_out.at[which, c // in_band]).start()

    def out_finish(which, land, out, n):
        count = in_band * (peers - 1) * lc
        whole(land, count, out_send.at[which], out_recv.at[which, n]).wait_recv()
        own = land.at[:, :, pl.ds(0, in_band * lc), :]
        pltpu.make_async_copy(own, own, own_out.at[which, n]).wait()
        modes = slice(n * band, (n + 1) * band)
        for l in range(layers):
            for f in range(face):
                out[l, f, :, modes] = land[l, f, modes].T

    in_start(0)
    for n in range(1, bands):
        turn(n)

    @pl.when(jnp.logical_not(has_low))
    def _():
        halo_low[...] = jnp.zeros_like(halo_low)

    @pl.when(jnp.logical_not(has_up))
    def _():
        halo_up[...] = jnp.zeros_like(halo_up)

    turns = list(reversed(range(groups))) if RELAYED_GROUP else list(range(groups))

    def land(c, g):
        whole(src, (peers - 1) * lc, in_send.at[0], in_recv.at[c, g], per).wait_recv()
        halo_start(0, c, g)

    items = schedule(chunks)

    def build(e, carry):
        for load in loads(e):
            load.wait()
        prepare(raw, e, lax.rem(e, SLOTS), modes_dev, adj, masks, w_hi, w_lo)

        @pl.when(e + SLOTS < elements)
        def _():
            for load in loads(e + SLOTS):
                load.start()

        if chunks > 1:

            @pl.when(e == SECOND)
            def _():
                in_start(1)

        for place, g in enumerate(turns):

            @pl.when(e == elements - groups + place - EARLY)
            def _():
                if place == 0:
                    own_copy(0).wait()
                land(0, g)

        return carry

    with jax.named_scope('build'):
        lax.fori_loop(0, elements, build, 0)

    def halves(value):
        high = value.astype(jnp.bfloat16)
        return high, (value - high.astype(jnp.float32)).astype(jnp.bfloat16)

    def product(a, l, f, lo, hi):
        def dot(left, right):
            return lax.dot_general(left, right, (((1,), (0,)), ((), ())), preferred_element_type=jnp.float32)

        y = dot(a, w_hi[l, f, lo:hi])
        return y[:rows] + y[rows:] + dot(a[:rows], w_lo[l, f, lo:hi])

    def keep_split(c, l, f, value):
        high, low = halves(value)
        split[c, l, :rows, f * blk : (f + 1) * blk] = high
        split[c, l, rows:, f * blk : (f + 1) * blk] = low

    sigma = THETA / DELTA
    last = (DEGREE - 1) % 2
    ratios = [1.0 / sigma]
    for _ in range(DEGREE):
        ratios.append(1.0 / (2.0 * sigma - ratios[-1]))

    def item(i):
        found = [jnp.int32(-1)] * 4
        for at, entry in enumerate(items):
            found = [jnp.where(i == at, value, old) for value, old in zip(entry, found)]
        return found

    def side(c, l, f, halo, t):
        if 0 <= l < layers:
            return split[c, l, :, f * blk : (f + 1) * blk]
        return jnp.concatenate(halves(halo[t, c, f]), axis=0)

    def advance(i, carry):
        t, c, t_next, c_next = item(i)

        @pl.when(t < 0)
        def _():
            @pl.when(c > 0)
            def _():
                with jax.named_scope('land'):
                    own_copy(c).wait()
                    for g in turns:
                        land(c, g)

            @pl.when(c == min(1, chunks - 1))
            def _():
                for late in range(2, chunks):
                    in_start(late)

            for l in range(layers):
                for f in range(face):
                    d = direction[0, c, l, f]
                    res[c, l, f] = d
                    x[0, c, l, f] = d
                    keep_split(c, l, f, d)

        now = lax.rem(t + 2, 2)
        keep, add = jnp.float32(0.0), jnp.float32(0.0)
        for at in range(DEGREE - 1):
            keep = jnp.where(t == at, jnp.float32(ratios[at + 1] * ratios[at]), keep)
            add = jnp.where(t == at, jnp.float32(2.0 * ratios[at + 1] / DELTA), add)

        for g in range(groups):

            @pl.when(t >= 0)
            def _():
                with jax.named_scope(f'wait{g}'):
                    halo_arrived(t, c, g)

                if g == 0:

                    @pl.when(t > 0)
                    def _():
                        halo_sent(t - 1, c)

                for f in range(g * per, (g + 1) * per):
                    ys = []
                    for l in range(layers):
                        a = jnp.concatenate([side(c, l - 1, f, halo_low, t), side(c, l + 1, f, halo_up, t)], axis=1)
                        ys.append(acc[c, l, f] + product(a, l, f, face * blk, inner))
                    for l, y in enumerate(ys):
                        d = direction[now, c, l, f]
                        total = d + y[:, :blk]
                        for b in range(bits):
                            term = y[:, (b + 1) * blk : (b + 2) * blk]
                            total = total + jnp.concatenate(
                                [term[(h ^ (1 << b)) * lc : ((h ^ (1 << b)) + 1) * lc] for h in range(peers)], axis=0
                            )
                        r = res[c, l, f] - total
                        res[c, l, f] = r
                        d_new = keep * d + add * r
                        direction[1 - now, c, l, f] = d_new
                        x[1 - now, c, l, f] = x[now, c, l, f] + d_new
                        keep_split(c, l, f, d_new)

                @pl.when(t < DEGREE - 1)
                def _():
                    halo_start(t + 1, c, g)

                @pl.when(t == DEGREE - 1)
                def _():
                    out_start(1, res, r_land, c, pl.ds(g * per, per))

        @pl.when(t == DEGREE - 2)
        def _():
            out_start(0, x.at[last], x_land, c)

        @pl.when(t < DEGREE - 1)
        def _():
            for l in range(layers):
                a = split[c, l]
                for f in range(face):
                    acc[c, l, f] = product(a, l, f, 0, face * blk)

        @pl.when(t_next >= 0)
        def _():
            with jax.named_scope('fwd'):
                halo_forward(t_next, c_next)

        return carry

    lax.fori_loop(0, len(items), advance, 0)

    with jax.named_scope('sent'):
        for c in range(chunks):
            halo_sent(DEGREE - 1, c)
        everything = (peers - 1) * chunks * lc
        whole(src, everything, in_send.at[0], in_recv.at[0, 0]).wait_send()
        if relayed:

            @pl.when(jnp.logical_or(both(odd, s >= 3), both(even, s < spaces - 3)))
            def _():
                pltpu.make_async_remote_copy(
                    src_ref=relay, dst_ref=relay, send_sem=forward_send.at[0], recv_sem=forward_recv.at[0, 0],
                    device_id={"space": s + jnp.where(odd, -1, 1)}, device_id_type=MESH,
                ).wait_send()

    for n in range(bands):
        with jax.named_scope(f'finx{n}'):
            out_finish(0, x_land, x_out, n)
        with jax.named_scope(f'finr{n}'):
            out_finish(1, r_land, r_out, n)
    with jax.named_scope('end'):
        for which, land, out in ((0, x_land, x_out), (1, r_land, r_out)):
            whole(land, everything, out_send.at[which], out_recv.at[which, 0]).wait_send()


def deliver(x, r, x_out, r_out, sem):
    copies = [pltpu.make_async_copy(x, x_out, sem.at[0]), pltpu.make_async_copy(r, r_out, sem.at[1])]
    for copy in copies:
        copy.start()
    for copy in copies:
        copy.wait()


def per_device(peers, spaces, source_field, mean_operator, field_operators, adjacency, mode_masks):
    layers, face, blk, modes_dev = source_field.shape
    bits = peers.bit_length() - 1
    chunks = CHUNKS
    while modes_dev % (peers * chunks * 8):
        chunks //= 2
    rows = modes_dev // chunks
    groups = 2 if face % 2 == 0 else 1
    weights = pltpu.VMEM((layers, face, (face + 2) * blk, (bits + 1) * blk), jnp.bfloat16)
    out = pltpu.VMEM(source_field.shape, jnp.float32)
    landing = pltpu.VMEM((layers, face, modes_dev, blk), jnp.float32)
    bands = min(chunks, max(modes_dev // 128, 1))
    field = (chunks, layers, face, rows, blk)
    halo = pltpu.VMEM((DEGREE, chunks, face, rows, blk), jnp.float32)
    dma = pltpu.SemaphoreType.DMA
    x, r = pl.pallas_call(
        functools.partial(solve_kernel, peers, spaces, chunks, modes_dev),
        in_specs=[
            pl.BlockSpec(memory_space=pl.ANY),
            pl.BlockSpec(memory_space=pl.ANY),
            pl.BlockSpec(memory_space=pl.ANY),
            pl.BlockSpec(memory_space=pltpu.SMEM),
            pl.BlockSpec(memory_space=pltpu.SMEM),
        ],
        out_specs=(pl.BlockSpec(memory_space=pltpu.VMEM), pl.BlockSpec(memory_space=pltpu.VMEM)),
        out_shape=(out, out),
        scratch_shapes=[
            pltpu.VMEM((SLOTS, 1 + field_operators.shape[0]) + mean_operator.shape[2:], jnp.float32),
            weights,
            weights,
            pltpu.VMEM((2,) + field, jnp.float32),
            pltpu.VMEM(field, jnp.float32),
            pltpu.VMEM((2,) + field, jnp.float32),
            pltpu.VMEM((chunks, layers, 2 * rows, face * blk), jnp.bfloat16),
            pltpu.VMEM((chunks, layers, face, rows, (bits + 1) * blk), jnp.float32),
            halo,
            halo,
            pltpu.VMEM((DEGREE, chunks, face // groups, rows, blk), jnp.float32),
            pltpu.VMEM(source_field.shape, jnp.float32),
            landing,
            landing,
            landing,
            dma((SLOTS, 2)),
            dma((bands,)),
            dma((chunks,)),
            dma((1,)),
            dma((chunks, groups)),
            dma((2, chunks, groups)),
            dma((2, chunks, groups)),
            dma((2, chunks, groups)),
            dma((2, chunks, groups)),
            dma((2, chunks)),
            dma((2, chunks)),
            dma((1,)),
            dma((2, chunks)),
            dma((2,)),
            dma((2, bands)),
            dma((2, bands)),
        ],
        compiler_params=pltpu.CompilerParams(
            collective_id=0, has_side_effects=True, vmem_limit_bytes=VMEM_LIMIT
        ),
    )(source_field, mean_operator, field_operators, adjacency, mode_masks)
    return x, r


def solution(mesh):
    in_specs = (
        P("space", None, None, "mode"),
        P("space", None, None, None),
        P(None, "space", None, None, None),
        P("space", None, None),
        P(),
    )
    out_specs = (P("space", None, None, "mode"), P("space", None, None, "mode"))
    return jax.shard_map(
        functools.partial(per_device, mesh.shape["mode"], mesh.shape["space"]),
        mesh=mesh, in_specs=in_specs, out_specs=out_specs, check_vma=False,
    )
```
